32 devices in a mesh: groups: 2 (over y), rows: 8 (over z, x), cols: 2 (over core).
Axes of the slice: x: 2, y: 2, z: 4, core: 2. Of those that a mesh axis runs over, the one named last changes fastest.
Arguments:
- series_a: float32 [4, 8192], P(None, ('groups', 'rows')), parts along dimension 1, may hold values from -100 to 100
- series_b: float32 [4, 2048], P(None, ('groups', 'rows', 'cols')), parts along dimension 1, may hold values from -100 to 100
- a_offsets: int32 [16], P(('groups', 'rows')), parts along dimension 0, may hold values from 0 to 511
- b_offsets: int32 [4], P(('groups', 'cols')), parts along dimension 0, may hold values from 0 to 511
Outputs:
- a_profile: float32 [8192, 16], P(('groups', 'rows', 'cols')), parts along dimension 0
- b_profile: float32 [4, 512, 16], P(('groups', 'cols'), 'rows'), parts along dimension 0
The draws below stay inside these ranges and needn't reach their ends.
There are 2 independent parts, one for each index of `groups`. The reference program is written for one: setup_inputs(seed, part) draws one part's arguments, and reference() takes and returns one part's arrays. A program takes and returns all parts, laid end to end along the dimension named above; each array names one. Nothing has to cross between parts.
All inputs are finite; a program needn't handle non-finite values.
Results may differ from the reference program's by a relative error of at most 0.00046.
Values sent between devices are 32-bit elements; how exact they have to be, the bound alone decides.
A program may use at most 64 MiB of HBM per device.

```python
import math
import jax
import jax.numpy as jnp
from jax import lax

C = 4
M = 512
K = 16
NA = 512
NB = 512
TA = 4096
TB = 1024
N_ROWS = 8
N_COLS = 2


def unit_spread(values):
    centred = values - jnp.mean(values, axis=1, keepdims=True)
    return centred / jnp.sqrt(jnp.mean(centred * centred, axis=1, keepdims=True) + 1e-06)


def smoothed(raw_values):
    breadth = max(1, M // 16)
    summed = raw_values
    for offset_step in range(1, breadth):
        summed = summed + jnp.roll(raw_values, offset_step, axis=1)
    return unit_spread(summed) + 0.25 * unit_spread(raw_values)


def base_series(key):
    noise_key = jax.random.fold_in(key, 101)
    scale_key = jax.random.fold_in(key, 102)
    factor_key = jax.random.fold_in(key, 103)
    noise = jnp.clip(jax.random.normal(noise_key, (C, TA), jnp.float32), -4.0, 4.0)
    scales = jnp.exp(jax.random.uniform(scale_key, (C, 1), jnp.float32, math.log(0.5), math.log(4.0)))
    factor = jnp.exp(jax.random.uniform(factor_key, (C, TA), jnp.float32, -0.7, 0.7))
    shaped = smoothed(noise * factor)
    return shaped * scales


def draw_series_a(key, part):
    return base_series(key)


def draw_series_b(key, part):
    source = base_series(key)
    sources = jax.random.randint(jax.random.fold_in(key, 303), (TB // M,), 0, TA)
    positions = ((sources[:, None] + jnp.arange(M)[None, :]) % TA).reshape(-1)
    copied = source[:, positions]
    centre = source - jnp.mean(source, axis=1, keepdims=True)
    spread = jnp.sqrt(jnp.mean(centre * centre, axis=1, keepdims=True))
    noise = jnp.clip(jax.random.normal(jax.random.fold_in(key, 304), (C, TB), jnp.float32), -4.0, 4.0)
    return copied + 0.35 * spread * noise


def touch_ends(values, rng, least, largest):
    index_at = [jax.random.randint(jax.random.fold_in(rng, axis), (), 0, length) for axis, length in enumerate(values.shape)]
    longest = values.shape.index(max(values.shape))
    next_to = index_at[:longest] + [(index_at[longest] + 1) % values.shape[longest]] + index_at[longest + 1:]
    return values.at[tuple(index_at)].set(least).at[tuple(next_to)].set(largest)


def setup_inputs(seed: int = 0, part: int = 0) -> dict:
    key_of = jax.random.split(jax.random.key(seed), 5)
    own_keys = jax.random.split(jax.random.fold_in(key_of[4], part), 5)
    return {
        "series_a": draw_series_a(jax.random.fold_in(jax.random.fold_in(key_of[4], part), 71), part),
        "series_b": draw_series_b(jax.random.fold_in(jax.random.fold_in(key_of[4], part), 71), part),
        "a_offsets": touch_ends(jax.random.randint(own_keys[2], (N_ROWS,), 0, M), jax.random.fold_in(own_keys[2], 1), 0, M - 1).astype(jnp.int32),
        "b_offsets": jax.random.randint(own_keys[3], (N_COLS,), 0, M).astype(jnp.int32),
    }


def normalize(series, starts):
    extent = series.shape[1]
    positions = (starts[:, None] + jnp.arange(M, dtype=jnp.int32)[None, :]) % extent
    pieces = []
    for channel in range(series.shape[0]):
        window = series[channel][positions]
        centred = window - lax.optimization_barrier(jnp.mean(window, axis=1, keepdims=True))
        spread = lax.optimization_barrier(jnp.mean(centred * centred, axis=1, keepdims=True))
        pieces.append((centred * lax.rsqrt(spread + 1e-05)).astype(jnp.bfloat16))
    return jnp.concatenate(pieces, axis=1)

def reference(series_a, series_b, a_offsets, b_offsets):
    b_starts = ((jnp.arange(N_COLS, dtype=jnp.int32) * NB + b_offsets)[:, None] + jnp.arange(NB, dtype=jnp.int32)[None, :]).reshape(-1)
    right_rows = normalize(series_b, b_starts)
    factor = 1.0 / (C * M)

    def one_block(best_rows, row_index):
        starts = row_index * NA - M + a_offsets[row_index] + jnp.arange(NA, dtype=jnp.int32)
        left_rows = normalize(series_a, starts)
        scores = jnp.dot(left_rows, right_rows.T, preferred_element_type=jnp.float32) * factor
        a_top = lax.top_k(scores, K)[0]
        b_top = lax.top_k(scores.T, K)[0]
        best_rows = lax.top_k(jnp.concatenate([best_rows, b_top], axis=1), K)[0]
        return (best_rows, a_top)
    start_rows = jnp.full((NB * N_COLS, K), -2.0, jnp.float32)
    best_rows, a_tops = lax.scan(one_block, start_rows, jnp.arange(N_ROWS, dtype=jnp.int32))
    return (a_tops.reshape(NA * N_ROWS, K), best_rows.reshape(N_COLS, NB, K))
```

```python
import functools

import jax
import jax.numpy as jnp
from jax import lax
from jax.experimental import pallas as pl
from jax.experimental.pallas import tpu as pltpu
from jax.sharding import PartitionSpec as P

M = 512
K = 16
NA = 512
NB = 512
LANES = 128
SUB = 8
SPAN = NA + M
WIDE = SPAN - LANES
MESH = pl.DeviceIdType.MESH


def comparators(n):
    pairs = []
    p = 1
    while p < n:
        k = p
        while k >= 1:
            for j in range(k % p, n - k, 2 * k):
                for i in range(min(k, n - j - k)):
                    if (i + j) // (2 * p) == (i + j + k) // (2 * p):
                        pairs.append((i + j, i + j + k))
            k //= 2
        p *= 2
    return pairs


def sort_desc(x):
    x = list(x)
    for i, j in comparators(len(x)):
        x[i], x[j] = jnp.maximum(x[i], x[j]), jnp.minimum(x[i], x[j])
    return x


def merge_top(a, b):
    n = len(a)
    x = [jnp.maximum(a[j], b[n - 1 - j]) for j in range(n)]
    d = n // 2
    while d >= 1:
        for j in range(n):
            if not j & d:
                x[j], x[j + d] = jnp.maximum(x[j], x[j + d]), jnp.minimum(x[j], x[j + d])
        d //= 2
    return x


def merge_sublanes(x):
    n = x[0].shape[0]
    while n > SUB:
        n //= 2
        x = merge_top([v[:n] for v in x], [v[n:] for v in x])
    d = n // 2
    while d >= 1:
        x = merge_top(x, [pltpu.roll(v, d, 0) for v in x])
        d //= 2
    return [v[0:1] for v in x]


def column_lists(ref, lanes):
    rows = ref.shape[0]
    lists = None
    for base in range(0, rows, K * SUB):
        group = sort_desc([ref[pl.ds(base + SUB * v, SUB), lanes] for v in range(K)])
        lists = group if lists is None else merge_top(lists, group)
    return lists


def hankel(segment, h_ref):
    sums = []
    sub = lax.broadcasted_iota(jnp.int32, (SUB, SPAN), 0)
    for c in range(segment.shape[0]):
        t = jnp.broadcast_to(segment[c : c + 1], (SUB, SPAN))
        for bit in (1, 2, 4):
            t = jnp.where((sub & bit) != 0, pltpu.roll(t, SPAN - bit, 1), t)
        total = None
        for b in range(LANES // SUB):
            piece = t if b == 0 else pltpu.roll(t, SPAN - SUB * b, 1)
            piece = piece[:, :WIDE]
            h_ref[c, SUB * b : SUB * b + SUB, :] = piece
            total = piece if total is None else total + piece
        sums.append(jnp.sum(total, axis=0, keepdims=True))
    return sums


def unit_stats(h_ref, sums):
    found = []
    parts = range(M // LANES)
    for c in range(len(sums)):
        centre = sums[c] * (1.0 / LANES)
        about = jnp.broadcast_to(centre, (SUB, WIDE))

        def squares(b, total):
            d = h_ref[c, pl.ds(pl.multiple_of(b * SUB, SUB), SUB), :] - about
            return total + d * d

        total = lax.fori_loop(0, LANES // SUB, squares, jnp.zeros((SUB, WIDE), jnp.float32), unroll=16)
        within = jnp.sum(total, axis=0, keepdims=True)
        means = [centre[:, LANES * q : LANES * q + NA] for q in parts]
        mean = sum(means[1:], means[0]) * (LANES / M)
        spread = sum(within[:, LANES * q : LANES * q + NA] for q in parts)
        for v in means:
            spread = spread + LANES * ((v - mean) * (v - mean))
        found.append((mean, lax.rsqrt(spread * (1.0 / M) + 1e-05)))
    return found


def normalise_rows(padded, offset, h_ref, spread_ref, left):
    channels, extent = padded.shape
    segment = pltpu.roll(padded, lax.rem(extent - offset, extent), 1)[:, :SPAN]
    stats = unit_stats(h_ref, hankel(segment, h_ref))
    rest = jnp.concatenate([v for pair in stats for v in pair], axis=0)
    pieces = []
    for _ in range(3):
        pieces.append(rest.astype(jnp.bfloat16).astype(jnp.float32))
        rest = rest - pieces[-1]
    split = jnp.concatenate(pieces, axis=0).T.astype(jnp.bfloat16)
    kinds = 2 * channels
    shape = (3 * kinds, kinds * LANES)
    chosen = lax.broadcasted_iota(jnp.int32, shape, 0) % kinds == lax.broadcasted_iota(jnp.int32, shape, 1) // LANES
    spread_ref[...] = jnp.dot(
        split, jnp.where(chosen, 1.0, 0.0).astype(jnp.bfloat16), preferred_element_type=jnp.float32
    )

    @pl.loop(0, LANES // 16, unroll=True)
    def _(b):
        at = pl.multiple_of(b * 16, 16)
        for q in range(NA // LANES):
            row = pl.multiple_of(at + LANES * q, 16)
            for c in range(channels):
                mean = spread_ref[pl.ds(row, 16), 2 * c * LANES : (2 * c + 1) * LANES]
                scale = spread_ref[pl.ds(row, 16), (2 * c + 1) * LANES : (2 * c + 2) * LANES]
                for m in range(0, M, LANES):
                    w = h_ref[c, pl.ds(at, 16), LANES * q + m : LANES * q + m + LANES]
                    left[pl.ds(row, 16), M * c + m : M * c + m + LANES] = ((w - mean) * scale).astype(jnp.bfloat16)


def shifted(x, lanes):
    lanes %= x.shape[1]
    return x if lanes == 0 else pltpu.roll(x, lanes, 1)


def kernel(
    rows, cols, aoff_hbm, boff_hbm, a_hbm, b_hbm, a_out, b_out,
    aoff, boff, off_out, off_in, abuf, bbuf, ha, hb, left, right, spread_out, score, score_far, score_t,
    alist, blist, arecv, brecv,
    own_sem, off_send, off_recv, a_send, a_recv, b_send, b_recv, la_send, la_recv, lb_send, lb_recv,
):
    channels = a_hbm.shape[0]
    count = rows * cols
    half = rows // 2
    g = lax.axis_index("groups")
    r = lax.axis_index("rows")
    k = lax.axis_index("cols")
    me = r * cols + k

    def ahead(x, d, n):
        d %= n
        y = x + d
        return y if d == 0 else jnp.where(y >= n, y - n, y)

    across = [ahead(k, d, cols) for d in range(cols)]
    if rows & (rows - 1):
        along = [ahead(r, d, rows) for d in range(rows)]
    else:
        along = [r ^ d for d in range(rows)]
    peers = [(i, j) for i in along[::-1] for j in across[::-1]][:-1]

    own_a = pltpu.make_async_copy(a_hbm, abuf.at[1], own_sem.at[0])
    own_b = pltpu.make_async_copy(b_hbm, bbuf.at[me], own_sem.at[1])
    offset_a = pltpu.make_async_copy(aoff_hbm, aoff, own_sem.at[2])
    offset_b = pltpu.make_async_copy(boff_hbm, boff, own_sem.at[3])
    for copy in (offset_a, own_a, own_b, offset_b):
        copy.start()

    barrier = pltpu.get_barrier_semaphore()
    for i, j in peers:
        pl.semaphore_signal(barrier, inc=1, device_id=(g, i, j), device_id_type=MESH)
    offset_a.wait()
    off_out[...] = jnp.full(off_out.shape, aoff[0], jnp.int32)
    pl.semaphore_wait(barrier, count - 1)

    def remote(src, dst, send, recv, to):
        return pltpu.make_async_remote_copy(
            src_ref=src, dst_ref=dst, send_sem=send, recv_sem=recv, device_id=to, device_id_type=MESH
        )

    far = ahead(r, half, rows)
    a_copies = [
        remote(a_hbm, abuf.at[slot], a_send.at[slot], a_recv.at[slot], (g, ahead(r, -d, rows), k))
        for slot, d in ((0, -1), (2, 1), (4, half), (3, half - 1), (5, half + 1))
    ]
    b_copies = [
        remote(b_hbm, bbuf.at[me], b_send.at[d], b_recv.at[me], (g, i, j)) for d, (i, j) in enumerate(peers)
    ]
    off_copy = remote(off_out, off_in, off_send.at[0], off_recv.at[0], (g, far, k))
    for copy in a_copies[:2] + b_copies + [off_copy] + a_copies[2:]:
        copy.start()

    own_a.wait()
    for copy in a_copies[:2]:
        copy.wait_recv()
    padded = jnp.concatenate([abuf[0], abuf[1], abuf[2]], axis=1)
    normalise_rows(padded, aoff[0], ha.at[0], spread_out.at[0], left.at[0])

    off_copy.wait_recv()
    for copy in a_copies[2:]:
        copy.wait_recv()
    padded = jnp.concatenate([abuf[3], abuf[4], abuf[5]], axis=1)
    normalise_rows(padded, jnp.max(off_in[...]), ha.at[1], spread_out.at[1], left.at[1])

    own_b.wait()
    offset_b.wait()
    for d, (i, j) in enumerate(peers):
        source = i * cols + j
        remote(b_hbm, bbuf.at[source], b_send.at[d], b_recv.at[source], (g, i, j)).wait_recv()
    whole = jnp.concatenate([bbuf[p] for p in range(count)], axis=1)
    extent_b = whole.shape[1]
    start = lax.rem(k * NB + boff[0], extent_b)
    segment_b = pltpu.roll(whole, lax.rem(extent_b - start, extent_b), 1)
    stats_b = unit_stats(hb, hankel(segment_b, hb))
    for c in range(channels):
        mean16 = jnp.broadcast_to(stats_b[c][0], (16, NB))
        scale16 = jnp.broadcast_to(stats_b[c][1], (16, NB))

        @pl.loop(0, LANES // 16, unroll=True)
        def _(b):
            at = pl.multiple_of(b * 16, 16)
            for q in range(M // LANES):
                w = hb[c, pl.ds(at, 16), LANES * q : LANES * q + NB]
                right[pl.ds(pl.multiple_of(at + M * c + LANES * q, 16), 16), :] = (
                    (w - mean16) * scale16
                ).astype(jnp.bfloat16)

    factor = 1.0 / (channels * M)
    score[...] = jnp.dot(left[0], right[...], preferred_element_type=jnp.float32) * factor
    reach = NB // 2
    side = r // half
    base = pl.multiple_of(side * reach, LANES)
    score_far[...] = jnp.dot(left[1], right[:, pl.ds(base, reach)], preferred_element_type=jnp.float32) * factor

    share_b = NB // rows
    per = LANES // share_b
    depth = K // per
    block = lax.broadcasted_iota(jnp.int32, (depth, LANES), 1) // share_b
    lb_copies = []
    for t in range(reach // LANES):
        near_list = column_lists(score, pl.ds(pl.multiple_of(base + LANES * t, LANES), LANES))
        far_list = column_lists(score_far, pl.ds(LANES * t, LANES))
        found = jnp.concatenate(merge_sublanes(merge_top(near_list, far_list)), axis=0)
        for u in range(per):
            packed = None
            for v in range(per):
                piece = shifted(found[depth * v : depth * v + depth], (v - u) * share_b)
                packed = piece if packed is None else jnp.where(block == v, piece, packed)
            blist[t * per + u] = packed
    low = side * half
    mine = r - low
    for d in range(1, half):
        to = mine ^ d if half & (half - 1) == 0 else ahead(mine, d, half)
        lb_copies.append(remote(blist.at[to], brecv.at[mine], lb_send.at[d], lb_recv.at[mine], (g, low + to, k)))
        lb_copies[-1].start()
    brecv[mine] = blist[mine]

    score_t[...] = score[...].T
    share_a = NA // cols
    for t in range(NA // LANES):
        found = jnp.concatenate(merge_sublanes(column_lists(score_t, pl.ds(LANES * t, LANES))), axis=0)
        alist[(LANES * t) // share_a, :, (LANES * t) % share_a : (LANES * t) % share_a + LANES] = found
    la_copies = []
    for d in range(1, cols):
        to = across[d]
        la_copies.append(remote(alist.at[to], arecv.at[k], la_send.at[d], la_recv.at[k], (g, r, to)))
        la_copies[-1].start()

    for d in range(1, half):
        source = mine ^ d if half & (half - 1) == 0 else ahead(mine, d, half)
        remote(blist.at[source], brecv.at[source], lb_send.at[d], lb_recv.at[source], (g, low + source, k)).wait_recv()
    lists = [brecv[:, j % depth, (j // depth) * share_b : (j // depth + 1) * share_b] for j in range(K)]
    b_out[...] = jnp.concatenate(merge_sublanes(lists), axis=0)

    held = alist[k]
    best = [held[j : j + 1] for j in range(K)]
    for d in range(1, cols):
        source = across[d]
        remote(alist.at[source], arecv.at[source], la_send.at[d], la_recv.at[source], (g, r, source)).wait_recv()
        came = arecv[source]
        best = merge_top(best, [came[j : j + 1] for j in range(K)])
    a_out[...] = jnp.concatenate(best, axis=0)

    for copy in a_copies + b_copies + [off_copy] + lb_copies + la_copies:
        copy.wait_send()


def local(rows, cols, series_a, series_b, a_offsets, b_offsets):
    channels, length_a = series_a.shape
    length_b = series_b.shape[1]
    count = rows * cols
    share_a = NA // cols
    share_b = NB // rows
    vmem = pl.BlockSpec(memory_space=pltpu.VMEM)
    hbm = pl.BlockSpec(memory_space=pltpu.HBM)
    dma = pltpu.SemaphoreType.DMA
    f32 = jnp.float32
    a_best, b_best = pl.pallas_call(
        functools.partial(kernel, rows, cols),
        out_shape=(
            pltpu.VMEM((K, share_a), f32),
            pltpu.VMEM((K, share_b), f32),
        ),
        in_specs=[hbm] * 4,
        out_specs=(vmem, vmem),
        scratch_shapes=[
            pltpu.SMEM((1,), jnp.int32),
            pltpu.SMEM((1,), jnp.int32),
            pltpu.VMEM((SUB, LANES), jnp.int32),
            pltpu.VMEM((SUB, LANES), jnp.int32),
            pltpu.VMEM((6, channels, length_a), f32),
            pltpu.VMEM((count, channels, length_b), f32),
            pltpu.VMEM((2, channels, LANES, WIDE), f32),
            pltpu.VMEM((channels, LANES, WIDE), f32),
            pltpu.VMEM((2, NA, channels * M), jnp.bfloat16),
            pltpu.VMEM((channels * M, NB), jnp.bfloat16),
            pltpu.VMEM((2, NA, 2 * channels * LANES), f32),
            pltpu.VMEM((NA, NB), f32),
            pltpu.VMEM((NA, NB // 2), f32),
            pltpu.VMEM((NB, NA), f32),
            pltpu.VMEM((cols, K, share_a), f32),
            pltpu.VMEM((rows // 2, K * share_b // LANES, LANES), f32),
            pltpu.VMEM((cols, K, share_a), f32),
            pltpu.VMEM((rows // 2, K * share_b // LANES, LANES), f32),
            dma((4,)),
            dma((1,)),
            dma((1,)),
            dma((6,)),
            dma((6,)),
            dma((count,)),
            dma((count,)),
            dma((cols,)),
            dma((cols,)),
            dma((rows // 2,)),
            dma((rows // 2,)),
        ],
        compiler_params=pltpu.CompilerParams(collective_id=0, has_side_effects=True),
        name="join",
    )(a_offsets, b_offsets, series_a, series_b)
    return (a_best.T, b_best.T[None])


def solution(mesh):
    in_specs = (
        P(None, ("groups", "rows")),
        P(None, ("groups", "rows", "cols")),
        P(("groups", "rows")),
        P(("groups", "cols")),
    )
    out_specs = (P(("groups", "rows", "cols"), None), P(("groups", "cols"), "rows", None))
    body = functools.partial(local, mesh.shape["rows"], mesh.shape["cols"])
    return jax.shard_map(body, mesh=mesh, in_specs=in_specs, out_specs=out_specs, check_vma=False)
```

```python
import functools

import jax
import jax.numpy as jnp
from jax import lax
from jax.experimental import pallas as pl
from jax.experimental.pallas import tpu as pltpu
from jax.sharding import PartitionSpec as P

M = 512
K = 16
NA = 512
NB = 512
LANES = 128
SUB = 8
SPAN = NA + M
WIDE = SPAN - LANES
MESH = pl.DeviceIdType.MESH


def comparators(n):
    pairs = []
    p = 1
    while p < n:
        k = p
        while k >= 1:
            for j in range(k % p, n - k, 2 * k):
                for i in range(min(k, n - j - k)):
                    if (i + j) // (2 * p) == (i + j + k) // (2 * p):
                        pairs.append((i + j, i + j + k))
            k //= 2
        p *= 2
    return pairs


def sort_desc(x):
    x = list(x)
    for i, j in comparators(len(x)):
        x[i], x[j] = jnp.maximum(x[i], x[j]), jnp.minimum(x[i], x[j])
    return x


def merge_top(a, b):
    n = len(a)
    x = [jnp.maximum(a[j], b[n - 1 - j]) for j in range(n)]
    d = n // 2
    while d >= 1:
        for j in range(n):
            if not j & d:
                x[j], x[j + d] = jnp.maximum(x[j], x[j + d]), jnp.minimum(x[j], x[j + d])
        d //= 2
    return x


def merge_sublanes(x):
    n = x[0].shape[0]
    while n > SUB:
        n //= 2
        x = merge_top([v[:n] for v in x], [v[n:] for v in x])
    d = n // 2
    while d >= 1:
        x = merge_top(x, [pltpu.roll(v, d, 0) for v in x])
        d //= 2
    return [v[0:1] for v in x]


def top_columns(ref, lanes):
    rows = ref.shape[0]
    lists = None
    for base in range(0, rows, K * SUB):
        group = sort_desc([ref[pl.ds(base + SUB * v, SUB), lanes] for v in range(K)])
        lists = group if lists is None else merge_top(lists, group)
    return merge_sublanes(lists)


def octets(segments, base_ref):
    for s in range(SUB):
        moved = segments if s == 0 else pltpu.roll(segments, SPAN - s, 1)
        for t in range(SPAN // LANES):
            base_ref[t, pl.ds(s, segments.shape[0], stride=SUB), :] = moved[:, LANES * t : LANES * t + LANES]


def hankel(base_ref, h_ref, c):
    rows = pl.ds(SUB * c, SUB)
    t = jnp.concatenate([base_ref[v, rows, :] for v in range(SPAN // LANES)], axis=1)
    for b in range(LANES // SUB):
        piece = t if b == 0 else pltpu.roll(t, SPAN - SUB * b, 1)
        h_ref[c, SUB * b : SUB * b + SUB, :] = piece[:, :WIDE]


def window_stats(segment):
    mean, squares, n = segment, None, 1
    step = M // 2
    while step >= 1:
        width = mean.shape[1]

        def pair(v):
            if step >= LANES:
                return v[:, : width - step], v[:, step:]
            return v, pltpu.roll(v, width - step, 1)

        a, b = pair(mean)
        gap = b - a
        mean = (a + b) * 0.5
        between = gap * gap * (0.5 * n)
        if squares is None:
            squares = between
        else:
            a, b = pair(squares)
            squares = (a + b) + between
        n *= 2
        step = step // 2
    return mean[:, :NA], lax.rsqrt(squares[:, :NA] * (1.0 / M) + 1e-05)


def shifted(x, lanes):
    lanes %= x.shape[1]
    return x if lanes == 0 else pltpu.roll(x, lanes, 1)


def kernel(
    rows, cols, aoff_hbm, boff_hbm, a_hbm, b_hbm, a_out, b_out,
    aoff, boff, abuf, bbuf, base, ha, left, right, spread_out, score, score_t, alist, blist, arecv, brecv,
    own_sem, a_send, a_recv, b_send, b_recv, la_send, la_recv, lb_send, lb_recv,
):
    channels = a_hbm.shape[0]
    count = rows * cols
    g = lax.axis_index("groups")
    r = lax.axis_index("rows")
    k = lax.axis_index("cols")
    me = r * cols + k

    def ahead(x, d, n):
        y = x + d
        return y if d == 0 else jnp.where(y >= n, y - n, y)

    if rows & (rows - 1):
        along = [ahead(r, d, rows) for d in range(rows)]
    else:
        along = [r ^ d for d in range(rows)]
    across = [ahead(k, d, cols) for d in range(cols)]
    peers = [(i, j) for i in along[::-1] for j in across[::-1]][:-1]

    own_a = pltpu.make_async_copy(a_hbm, abuf.at[1], own_sem.at[0])
    own_b = pltpu.make_async_copy(b_hbm, bbuf.at[me], own_sem.at[1])
    offset_a = pltpu.make_async_copy(aoff_hbm, aoff, own_sem.at[2])
    offset_b = pltpu.make_async_copy(boff_hbm, boff, own_sem.at[3])
    for copy in (own_a, own_b, offset_a, offset_b):
        copy.start()

    barrier = pltpu.get_barrier_semaphore()
    for i, j in peers:
        pl.semaphore_signal(barrier, inc=1, device_id=(g, i, j), device_id_type=MESH)
    pl.semaphore_wait(barrier, count - 1)

    after = ahead(r, 1, rows)
    before = ahead(r, rows - 1, rows)
    a_copies = [
        pltpu.make_async_remote_copy(
            src_ref=a_hbm, dst_ref=abuf.at[slot], send_sem=a_send.at[slot], recv_sem=a_recv.at[slot],
            device_id=(g, to, k), device_id_type=MESH,
        )
        for slot, to in ((0, after), (2, before))
    ]
    for copy in a_copies:
        copy.start()
    b_copies = []
    for d, (i, j) in enumerate(peers):
        b_copies.append(
            pltpu.make_async_remote_copy(
                src_ref=b_hbm, dst_ref=bbuf.at[me], send_sem=b_send.at[d], recv_sem=b_recv.at[me],
                device_id=(g, i, j), device_id_type=MESH,
            )
        )
        b_copies[-1].start()

    for copy in (own_a, offset_a, own_b, offset_b):
        copy.wait()
    for copy in a_copies:
        copy.wait_recv()
    for d, (i, j) in enumerate(peers):
        source = i * cols + j
        pltpu.make_async_remote_copy(
            src_ref=b_hbm, dst_ref=bbuf.at[source], send_sem=b_send.at[d], recv_sem=b_recv.at[source],
            device_id=(g, i, j), device_id_type=MESH,
        ).wait_recv()
    padded = jnp.concatenate([abuf[0], abuf[1], abuf[2]], axis=1)
    extent = padded.shape[1]
    segment = pltpu.roll(padded, lax.rem(extent - aoff[0], extent), 1)[:, :SPAN]
    whole = jnp.concatenate([bbuf[p] for p in range(count)], axis=1)
    extent_b = whole.shape[1]
    start = lax.rem(k * NB + boff[0], extent_b)
    segment_b = pltpu.roll(whole, lax.rem(extent_b - start, extent_b), 1)[:, :SPAN]
    segments = jnp.concatenate([segment, segment_b], axis=0)
    octets(segments, base)
    means, scales = window_stats(segments)

    rest = jnp.concatenate([means[:channels], scales[:channels]], axis=0)
    pieces = []
    for _ in range(3):
        pieces.append(rest.astype(jnp.bfloat16).astype(jnp.float32))
        rest = rest - pieces[-1]
    split = jnp.concatenate(pieces, axis=0).T.astype(jnp.bfloat16)
    kinds = 2 * channels
    shape = (3 * kinds, kinds * LANES)
    chosen = lax.broadcasted_iota(jnp.int32, shape, 0) % kinds == lax.broadcasted_iota(jnp.int32, shape, 1) // LANES
    spread_out[...] = jnp.dot(
        split, jnp.where(chosen, 1.0, 0.0).astype(jnp.bfloat16), preferred_element_type=jnp.float32
    )

    for c in range(channels):
        hankel(base, ha, c)
        hankel(base, ha, channels + c)
        for at in range(0, LANES, 16):
            for q in range(NA // LANES):
                row = at + LANES * q
                mean = spread_out[row : row + 16, c * LANES : (c + 1) * LANES]
                scale = spread_out[row : row + 16, (channels + c) * LANES : (channels + c + 1) * LANES]
                for m in range(0, M, LANES):
                    w = ha[c, at : at + 16, LANES * q + m : LANES * q + m + LANES]
                    left[row : row + 16, M * c + m : M * c + m + LANES] = ((w - mean) * scale).astype(jnp.bfloat16)
        mean16 = jnp.broadcast_to(means[channels + c : channels + c + 1], (16, NB))
        scale16 = jnp.broadcast_to(scales[channels + c : channels + c + 1], (16, NB))
        for at in range(0, LANES, 16):
            for q in range(M // LANES):
                w = ha[channels + c, at : at + 16, LANES * q : LANES * q + NB]
                row = at + M * c + LANES * q
                right[row : row + 16, :] = ((w - mean16) * scale16).astype(jnp.bfloat16)

    score[...] = jnp.dot(left[...], right[...], preferred_element_type=jnp.float32) * (1.0 / (channels * M))

    share_b = NB // rows
    per = LANES // share_b
    tiles = NB // LANES
    depth = K // per
    block = lax.broadcasted_iota(jnp.int32, (depth, LANES), 1) // share_b
    own = r // per
    place = r - own * per
    lb_copies = []

    def send_list(to):
        lb_copies.append(
            pltpu.make_async_remote_copy(
                src_ref=blist.at[to], dst_ref=brecv.at[r], send_sem=lb_send.at[len(lb_copies)], recv_sem=lb_recv.at[r],
                device_id=(g, to, k), device_id_type=MESH,
            )
        )
        lb_copies[-1].start()

    for n in range(tiles):
        if n == tiles - 1:
            t = own
        else:
            down = tiles - 1 - n
            t = jnp.where(
                2 * own < tiles - 1,
                jnp.where(own >= down, down - 1, down),
                jnp.where(own <= n, n + 1, n),
            )
        found = jnp.concatenate(top_columns(score, pl.ds(pl.multiple_of(LANES * t, LANES), LANES)), axis=0)
        for u in range(per):
            packed = None
            for v in range(per):
                piece = shifted(found[depth * v : depth * v + depth], (v - u) * share_b)
                packed = piece if packed is None else jnp.where(block == v, piece, packed)
            blist[t * per + u] = packed
        for u in range(per - 1 if n == tiles - 1 else per):
            send_list(t * per + (ahead(place, u + 1, per) if n == tiles - 1 else u))
    brecv[r] = blist[r]

    score_t[...] = score[...].T
    share_a = NA // cols
    for t in range(NA // LANES):
        found = jnp.concatenate(top_columns(score_t, pl.ds(LANES * t, LANES)), axis=0)
        alist[(LANES * t) // share_a, :, (LANES * t) % share_a : (LANES * t) % share_a + LANES] = found
    la_copies = []
    for d in range(1, cols):
        to = across[d]
        la_copies.append(
            pltpu.make_async_remote_copy(
                src_ref=alist.at[to], dst_ref=arecv.at[k], send_sem=la_send.at[d], recv_sem=la_recv.at[k],
                device_id=(g, r, to), device_id_type=MESH,
            )
        )
        la_copies[-1].start()

    for d in range(1, rows):
        source = ahead(r, d, rows)
        pltpu.make_async_remote_copy(
            src_ref=blist.at[source], dst_ref=brecv.at[source], send_sem=lb_send.at[d], recv_sem=lb_recv.at[source],
            device_id=(g, source, k), device_id_type=MESH,
        ).wait_recv()
    lists = [brecv[:, j % depth, (j // depth) * share_b : (j // depth + 1) * share_b] for j in range(K)]
    b_out[...] = jnp.concatenate(merge_sublanes(lists), axis=0)

    held = alist[k]
    best = [held[j : j + 1] for j in range(K)]
    for d in range(1, cols):
        source = across[d]
        pltpu.make_async_remote_copy(
            src_ref=alist.at[source], dst_ref=arecv.at[source], send_sem=la_send.at[d], recv_sem=la_recv.at[source],
            device_id=(g, r, source), device_id_type=MESH,
        ).wait_recv()
        came = arecv[source]
        best = merge_top(best, [came[j : j + 1] for j in range(K)])
    a_out[...] = jnp.concatenate(best, axis=0)

    for copy in a_copies + b_copies + lb_copies + la_copies:
        copy.wait_send()


def local(rows, cols, series_a, series_b, a_offsets, b_offsets):
    channels, length_a = series_a.shape
    length_b = series_b.shape[1]
    count = rows * cols
    share_a = NA // cols
    share_b = NB // rows
    vmem = pl.BlockSpec(memory_space=pltpu.VMEM)
    hbm = pl.BlockSpec(memory_space=pltpu.HBM)
    dma = pltpu.SemaphoreType.DMA
    f32 = jnp.float32
    a_best, b_best = pl.pallas_call(
        functools.partial(kernel, rows, cols),
        out_shape=(
            pltpu.VMEM((K, share_a), f32),
            pltpu.VMEM((K, share_b), f32),
        ),
        in_specs=[hbm] * 4,
        out_specs=(vmem, vmem),
        scratch_shapes=[
            pltpu.SMEM((1,), jnp.int32),
            pltpu.SMEM((1,), jnp.int32),
            pltpu.VMEM((3, channels, length_a), f32),
            pltpu.VMEM((count, channels, length_b), f32),
            pltpu.VMEM((SPAN // LANES, 2 * channels * SUB, LANES), f32),
            pltpu.VMEM((2 * channels, LANES, WIDE), f32),
            pltpu.VMEM((NA, channels * M), jnp.bfloat16),
            pltpu.VMEM((channels * M, NB), jnp.bfloat16),
            pltpu.VMEM((NA, 2 * channels * LANES), f32),
            pltpu.VMEM((NA, NB), f32),
            pltpu.VMEM((NB, NA), f32),
            pltpu.VMEM((cols, K, share_a), f32),
            pltpu.VMEM((rows, K * share_b // LANES, LANES), f32),
            pltpu.VMEM((cols, K, share_a), f32),
            pltpu.VMEM((rows, K * share_b // LANES, LANES), f32),
            dma((4,)),
            dma((3,)),
            dma((3,)),
            dma((count,)),
            dma((count,)),
            dma((cols,)),
            dma((cols,)),
            dma((rows,)),
            dma((rows,)),
        ],
        compiler_params=pltpu.CompilerParams(collective_id=0, has_side_effects=True),
        name="join",
    )(a_offsets, b_offsets, series_a, series_b)
    return (a_best.T, b_best.T[None])


def solution(mesh):
    in_specs = (
        P(None, ("groups", "rows")),
        P(None, ("groups", "rows", "cols")),
        P(("groups", "rows")),
        P(("groups", "cols")),
    )
    out_specs = (P(("groups", "rows", "cols"), None), P(("groups", "cols"), "rows", None))
    body = functools.partial(local, mesh.shape["rows"], mesh.shape["cols"])
    return jax.shard_map(body, mesh=mesh, in_specs=in_specs, out_specs=out_specs, check_vma=False)
```

```python
import functools

import jax
import jax.numpy as jnp
from jax import lax
from jax.experimental import pallas as pl
from jax.experimental.pallas import tpu as pltpu
from jax.sharding import PartitionSpec as P

M = 512
K = 16
NA = 512
NB = 512
LANES = 128
SUB = 8
SPAN = NA + M
WIDE = SPAN - LANES
MESH = pl.DeviceIdType.MESH


def comparators(n):
    pairs = []
    p = 1
    while p < n:
        k = p
        while k >= 1:
            for j in range(k % p, n - k, 2 * k):
                for i in range(min(k, n - j - k)):
                    if (i + j) // (2 * p) == (i + j + k) // (2 * p):
                        pairs.append((i + j, i + j + k))
            k //= 2
        p *= 2
    return pairs


def sort_desc(x):
    x = list(x)
    for i, j in comparators(len(x)):
        x[i], x[j] = jnp.maximum(x[i], x[j]), jnp.minimum(x[i], x[j])
    return x


def merge_top(a, b):
    n = len(a)
    x = [jnp.maximum(a[j], b[n - 1 - j]) for j in range(n)]
    d = n // 2
    while d >= 1:
        for j in range(n):
            if not j & d:
                x[j], x[j + d] = jnp.maximum(x[j], x[j + d]), jnp.minimum(x[j], x[j + d])
        d //= 2
    return x


def merge_sublanes(x):
    n = x[0].shape[0]
    while n > SUB:
        n //= 2
        x = merge_top([v[:n] for v in x], [v[n:] for v in x])
    d = n // 2
    while d >= 1:
        x = merge_top(x, [pltpu.roll(v, d, 0) for v in x])
        d //= 2
    return [v[0:1] for v in x]


def top_columns(ref, lanes):
    rows = ref.shape[0]
    lists = None
    for base in range(0, rows, K * SUB):
        group = sort_desc([ref[pl.ds(base + SUB * v, SUB), lanes] for v in range(K)])
        lists = group if lists is None else merge_top(lists, group)
    return merge_sublanes(lists)


def octets(segments, base_ref):
    for s in range(SUB):
        moved = segments if s == 0 else pltpu.roll(segments, SPAN - s, 1)
        for t in range(SPAN // LANES):
            base_ref[t, pl.ds(s, segments.shape[0], stride=SUB), :] = moved[:, LANES * t : LANES * t + LANES]


def hankel(base_ref, h_ref, c):
    rows = pl.ds(SUB * c, SUB)
    t = jnp.concatenate([base_ref[v, rows, :] for v in range(SPAN // LANES)], axis=1)
    for b in range(LANES // SUB):
        piece = t if b == 0 else pltpu.roll(t, SPAN - SUB * b, 1)
        h_ref[c, SUB * b : SUB * b + SUB, :] = piece[:, :WIDE]


def window_stats(segment):
    mean, squares, n = segment, None, 1
    step = M // 2
    while step >= 1:
        width = mean.shape[1]

        def pair(v):
            if step >= LANES:
                return v[:, : width - step], v[:, step:]
            return v, pltpu.roll(v, width - step, 1)

        a, b = pair(mean)
        gap = b - a
        mean = (a + b) * 0.5
        between = gap * gap * (0.5 * n)
        if squares is None:
            squares = between
        else:
            a, b = pair(squares)
            squares = (a + b) + between
        n *= 2
        step = step // 2
    return mean[:, :NA], lax.rsqrt(squares[:, :NA] * (1.0 / M) + 1e-05)


def shifted(x, lanes):
    lanes %= x.shape[1]
    return x if lanes == 0 else pltpu.roll(x, lanes, 1)


def kernel(
    rows, cols, aoff_hbm, boff_hbm, a_hbm, b_hbm, a_out, b_out,
    aoff, boff, abuf, bbuf, base, ha, left, right, spread_out, score, score_t, alist, blist, arecv, brecv,
    own_sem, a_send, a_recv, b_send, b_recv, la_send, la_recv, lb_send, lb_recv,
):
    channels = a_hbm.shape[0]
    count = rows * cols
    g = lax.axis_index("groups")
    r = lax.axis_index("rows")
    k = lax.axis_index("cols")
    me = r * cols + k

    def ahead(x, d, n):
        y = x + d
        return y if d == 0 else jnp.where(y >= n, y - n, y)

    if rows & (rows - 1):
        along = [ahead(r, d, rows) for d in range(rows)]
    else:
        along = [r ^ d for d in range(rows)]
    across = [ahead(k, d, cols) for d in range(cols)]
    peers = [(i, j) for i in along[::-1] for j in across[::-1]][:-1]

    own_a = pltpu.make_async_copy(a_hbm, abuf.at[1], own_sem.at[0])
    own_b = pltpu.make_async_copy(b_hbm, bbuf.at[me], own_sem.at[1])
    offset_a = pltpu.make_async_copy(aoff_hbm, aoff, own_sem.at[2])
    offset_b = pltpu.make_async_copy(boff_hbm, boff, own_sem.at[3])
    for copy in (own_a, own_b, offset_a, offset_b):
        copy.start()

    barrier = pltpu.get_barrier_semaphore()
    for i, j in peers:
        pl.semaphore_signal(barrier, inc=1, device_id=(g, i, j), device_id_type=MESH)
    pl.semaphore_wait(barrier, count - 1)

    after = ahead(r, 1, rows)
    before = ahead(r, rows - 1, rows)
    a_copies = [
        pltpu.make_async_remote_copy(
            src_ref=a_hbm, dst_ref=abuf.at[slot], send_sem=a_send.at[slot], recv_sem=a_recv.at[slot],
            device_id=(g, to, k), device_id_type=MESH,
        )
        for slot, to in ((0, after), (2, before))
    ]
    for copy in a_copies:
        copy.start()
    b_copies = []
    for d, (i, j) in enumerate(peers):
        b_copies.append(
            pltpu.make_async_remote_copy(
                src_ref=b_hbm, dst_ref=bbuf.at[me], send_sem=b_send.at[d], recv_sem=b_recv.at[me],
                device_id=(g, i, j), device_id_type=MESH,
            )
        )
        b_copies[-1].start()

    for copy in (own_a, offset_a, own_b, offset_b):
        copy.wait()
    for copy in a_copies:
        copy.wait_recv()
    for d, (i, j) in enumerate(peers):
        source = i * cols + j
        pltpu.make_async_remote_copy(
            src_ref=b_hbm, dst_ref=bbuf.at[source], send_sem=b_send.at[d], recv_sem=b_recv.at[source],
            device_id=(g, i, j), device_id_type=MESH,
        ).wait_recv()
    padded = jnp.concatenate([abuf[0], abuf[1], abuf[2]], axis=1)
    extent = padded.shape[1]
    segment = pltpu.roll(padded, lax.rem(extent - aoff[0], extent), 1)[:, :SPAN]
    whole = jnp.concatenate([bbuf[p] for p in range(count)], axis=1)
    extent_b = whole.shape[1]
    start = lax.rem(k * NB + boff[0], extent_b)
    segment_b = pltpu.roll(whole, lax.rem(extent_b - start, extent_b), 1)[:, :SPAN]
    segments = jnp.concatenate([segment, segment_b], axis=0)
    octets(segments, base)
    hankel(base, ha, 0)
    hankel(base, ha, channels)
    means, scales = window_stats(segments)

    rest = jnp.concatenate([means[:channels], scales[:channels]], axis=0)
    pieces = []
    for _ in range(3):
        pieces.append(rest.astype(jnp.bfloat16).astype(jnp.float32))
        rest = rest - pieces[-1]
    split = jnp.concatenate(pieces, axis=0).T.astype(jnp.bfloat16)
    kinds = 2 * channels
    shape = (3 * kinds, kinds * LANES)
    chosen = lax.broadcasted_iota(jnp.int32, shape, 0) % kinds == lax.broadcasted_iota(jnp.int32, shape, 1) // LANES
    spread_out[...] = jnp.dot(
        split, jnp.where(chosen, 1.0, 0.0).astype(jnp.bfloat16), preferred_element_type=jnp.float32
    )

    for c in range(channels):
        if c + 1 < channels:
            hankel(base, ha, c + 1)
            hankel(base, ha, channels + c + 1)
        for at in range(0, LANES, 16):
            for q in range(NA // LANES):
                row = at + LANES * q
                mean = spread_out[row : row + 16, c * LANES : (c + 1) * LANES]
                scale = spread_out[row : row + 16, (channels + c) * LANES : (channels + c + 1) * LANES]
                for m in range(0, M, LANES):
                    w = ha[c, at : at + 16, LANES * q + m : LANES * q + m + LANES]
                    left[row : row + 16, M * c + m : M * c + m + LANES] = ((w - mean) * scale).astype(jnp.bfloat16)
        mean16 = jnp.broadcast_to(means[channels + c : channels + c + 1], (16, NB))
        scale16 = jnp.broadcast_to(scales[channels + c : channels + c + 1], (16, NB))
        for at in range(0, LANES, 16):
            for q in range(M // LANES):
                w = ha[channels + c, at : at + 16, LANES * q : LANES * q + NB]
                row = at + M * c + LANES * q
                right[row : row + 16, :] = ((w - mean16) * scale16).astype(jnp.bfloat16)

    score[...] = jnp.dot(left[...], right[...], preferred_element_type=jnp.float32) * (1.0 / (channels * M))

    share_b = NB // rows
    per = LANES // share_b
    tiles = NB // LANES
    depth = K // per
    block = lax.broadcasted_iota(jnp.int32, (depth, LANES), 1) // share_b
    own = r // per
    place = r - own * per
    lb_copies = []

    def send_list(to):
        lb_copies.append(
            pltpu.make_async_remote_copy(
                src_ref=blist.at[to], dst_ref=brecv.at[r], send_sem=lb_send.at[len(lb_copies)], recv_sem=lb_recv.at[r],
                device_id=(g, to, k), device_id_type=MESH,
            )
        )
        lb_copies[-1].start()

    for n in range(tiles):
        if n == tiles - 1:
            t = own
        else:
            down = tiles - 1 - n
            t = jnp.where(
                2 * own < tiles - 1,
                jnp.where(own >= down, down - 1, down),
                jnp.where(own <= n, n + 1, n),
            )
        found = jnp.concatenate(top_columns(score, pl.ds(pl.multiple_of(LANES * t, LANES), LANES)), axis=0)
        for u in range(per):
            packed = None
            for v in range(per):
                piece = shifted(found[depth * v : depth * v + depth], (v - u) * share_b)
                packed = piece if packed is None else jnp.where(block == v, piece, packed)
            blist[t * per + u] = packed
        for u in range(per - 1 if n == tiles - 1 else per):
            send_list(t * per + (ahead(place, u + 1, per) if n == tiles - 1 else u))
    brecv[r] = blist[r]

    score_t[...] = score[...].T
    share_a = NA // cols
    for t in range(NA // LANES):
        found = jnp.concatenate(top_columns(score_t, pl.ds(LANES * t, LANES)), axis=0)
        alist[(LANES * t) // share_a, :, (LANES * t) % share_a : (LANES * t) % share_a + LANES] = found
    la_copies = []
    for d in range(1, cols):
        to = across[d]
        la_copies.append(
            pltpu.make_async_remote_copy(
                src_ref=alist.at[to], dst_ref=arecv.at[k], send_sem=la_send.at[d], recv_sem=la_recv.at[k],
                device_id=(g, r, to), device_id_type=MESH,
            )
        )
        la_copies[-1].start()

    held = alist[k]
    best = [held[j : j + 1] for j in range(K)]
    for d in range(1, cols):
        source = across[d]
        pltpu.make_async_remote_copy(
            src_ref=alist.at[source], dst_ref=arecv.at[source], send_sem=la_send.at[d], recv_sem=la_recv.at[source],
            device_id=(g, r, source), device_id_type=MESH,
        ).wait_recv()
        came = arecv[source]
        best = merge_top(best, [came[j : j + 1] for j in range(K)])
    a_out[...] = jnp.concatenate(best, axis=0)

    for d in range(1, rows):
        source = ahead(r, d, rows)
        pltpu.make_async_remote_copy(
            src_ref=blist.at[source], dst_ref=brecv.at[source], send_sem=lb_send.at[d], recv_sem=lb_recv.at[source],
            device_id=(g, source, k), device_id_type=MESH,
        ).wait_recv()
    lists = [brecv[:, j % depth, (j // depth) * share_b : (j // depth + 1) * share_b] for j in range(K)]
    b_out[...] = jnp.concatenate(merge_sublanes(lists), axis=0)

    for copy in a_copies + b_copies + lb_copies + la_copies:
        copy.wait_send()


def local(rows, cols, series_a, series_b, a_offsets, b_offsets):
    channels, length_a = series_a.shape
    length_b = series_b.shape[1]
    count = rows * cols
    share_a = NA // cols
    share_b = NB // rows
    vmem = pl.BlockSpec(memory_space=pltpu.VMEM)
    hbm = pl.BlockSpec(memory_space=pltpu.HBM)
    dma = pltpu.SemaphoreType.DMA
    f32 = jnp.float32
    a_best, b_best = pl.pallas_call(
        functools.partial(kernel, rows, cols),
        out_shape=(
            pltpu.VMEM((K, share_a), f32),
            pltpu.VMEM((K, share_b), f32),
        ),
        in_specs=[hbm] * 4,
        out_specs=(vmem, vmem),
        scratch_shapes=[
            pltpu.SMEM((1,), jnp.int32),
            pltpu.SMEM((1,), jnp.int32),
            pltpu.VMEM((3, channels, length_a), f32),
            pltpu.VMEM((count, channels, length_b), f32),
            pltpu.VMEM((SPAN // LANES, 2 * channels * SUB, LANES), f32),
            pltpu.VMEM((2 * channels, LANES, WIDE), f32),
            pltpu.VMEM((NA, channels * M), jnp.bfloat16),
            pltpu.VMEM((channels * M, NB), jnp.bfloat16),
            pltpu.VMEM((NA, 2 * channels * LANES), f32),
            pltpu.VMEM((NA, NB), f32),
            pltpu.VMEM((NB, NA), f32),
            pltpu.VMEM((cols, K, share_a), f32),
            pltpu.VMEM((rows, K * share_b // LANES, LANES), f32),
            pltpu.VMEM((cols, K, share_a), f32),
            pltpu.VMEM((rows, K * share_b // LANES, LANES), f32),
            dma((4,)),
            dma((3,)),
            dma((3,)),
            dma((count,)),
            dma((count,)),
            dma((cols,)),
            dma((cols,)),
            dma((rows,)),
            dma((rows,)),
        ],
        compiler_params=pltpu.CompilerParams(collective_id=0, has_side_effects=True),
        name="join",
    )(a_offsets, b_offsets, series_a, series_b)
    return (a_best.T, b_best.T[None])


def solution(mesh):
    in_specs = (
        P(None, ("groups", "rows")),
        P(None, ("groups", "rows", "cols")),
        P(("groups", "rows")),
        P(("groups", "cols")),
    )
    out_specs = (P(("groups", "rows", "cols"), None), P(("groups", "cols"), "rows", None))
    body = functools.partial(local, mesh.shape["rows"], mesh.shape["cols"])
    return jax.shard_map(body, mesh=mesh, in_specs=in_specs, out_specs=out_specs, check_vma=False)
```

```python
import functools

import jax
import jax.numpy as jnp
from jax import lax
from jax.experimental import pallas as pl
from jax.experimental.pallas import tpu as pltpu
from jax.sharding import PartitionSpec as P

M = 512
K = 16
NA = 512
NB = 512
LANES = 128
SUB = 8
SPAN = NA + M
WIDE = SPAN - LANES
MESH = pl.DeviceIdType.MESH


def comparators(n):
    pairs = []
    p = 1
    while p < n:
        k = p
        while k >= 1:
            for j in range(k % p, n - k, 2 * k):
                for i in range(min(k, n - j - k)):
                    if (i + j) // (2 * p) == (i + j + k) // (2 * p):
                        pairs.append((i + j, i + j + k))
            k //= 2
        p *= 2
    return pairs


def sort_desc(x):
    x = list(x)
    for i, j in comparators(len(x)):
        x[i], x[j] = jnp.maximum(x[i], x[j]), jnp.minimum(x[i], x[j])
    return x


def merge_top(a, b):
    n = len(a)
    x = [jnp.maximum(a[j], b[n - 1 - j]) for j in range(n)]
    d = n // 2
    while d >= 1:
        for j in range(n):
            if not j & d:
                x[j], x[j + d] = jnp.maximum(x[j], x[j + d]), jnp.minimum(x[j], x[j + d])
        d //= 2
    return x


def merge_sublanes(x):
    n = x[0].shape[0]
    while n > SUB:
        n //= 2
        x = merge_top([v[:n] for v in x], [v[n:] for v in x])
    d = n // 2
    while d >= 1:
        x = merge_top(x, [pltpu.roll(v, d, 0) for v in x])
        d //= 2
    return [v[0:1] for v in x]


def top_columns(ref, lanes):
    rows = ref.shape[0]
    lists = None
    for base in range(0, rows, K * SUB):
        group = sort_desc([ref[pl.ds(base + SUB * v, SUB), lanes] for v in range(K)])
        lists = group if lists is None else merge_top(lists, group)
    return merge_sublanes(lists)


def octets(segments, base_ref):
    for s in range(SUB):
        moved = segments if s == 0 else pltpu.roll(segments, SPAN - s, 1)
        for t in range(SPAN // LANES):
            base_ref[t, pl.ds(s, segments.shape[0], stride=SUB), :] = moved[:, LANES * t : LANES * t + LANES]


def hankel(base_ref, h_ref, c):
    rows = pl.ds(SUB * c, SUB)
    t = jnp.concatenate([base_ref[v, rows, :] for v in range(SPAN // LANES)], axis=1)
    for b in range(LANES // SUB):
        piece = t if b == 0 else pltpu.roll(t, SPAN - SUB * b, 1)
        h_ref[c, SUB * b : SUB * b + SUB, :] = piece[:, :WIDE]


def window_stats(segment):
    mean, squares, n = segment, None, 1
    step = M // 2
    while step >= 1:
        width = mean.shape[1]

        def pair(v):
            if step >= LANES:
                return v[:, : width - step], v[:, step:]
            return v, pltpu.roll(v, width - step, 1)

        a, b = pair(mean)
        gap = b - a
        mean = (a + b) * 0.5
        between = gap * gap * (0.5 * n)
        if squares is None:
            squares = between
        else:
            a, b = pair(squares)
            squares = (a + b) + between
        n *= 2
        step = step // 2
    return mean[:, :NA], lax.rsqrt(squares[:, :NA] * (1.0 / M) + 1e-05)


def shifted(x, lanes):
    lanes %= x.shape[1]
    return x if lanes == 0 else pltpu.roll(x, lanes, 1)


def kernel(
    rows, cols, aoff_hbm, boff_hbm, a_hbm, b_hbm, a_out, b_out,
    aoff, boff, abuf, bbuf, base, ha, left, right, spread_out, score, score_t, alist, blist, arecv, brecv,
    own_sem, a_send, a_recv, b_send, b_recv, la_send, la_recv, lb_send, lb_recv,
):
    channels = a_hbm.shape[0]
    count = rows * cols
    g = lax.axis_index("groups")
    r = lax.axis_index("rows")
    k = lax.axis_index("cols")
    me = r * cols + k

    def ahead(x, d, n):
        y = x + d
        return y if d == 0 else jnp.where(y >= n, y - n, y)

    if rows & (rows - 1):
        along = [ahead(r, d, rows) for d in range(rows)]
    else:
        along = [r ^ d for d in range(rows)]
    across = [ahead(k, d, cols) for d in range(cols)]
    peers = [(i, j) for i in along[::-1] for j in across[::-1]][:-1]

    barrier = pltpu.get_barrier_semaphore()
    for i, j in peers:
        pl.semaphore_signal(barrier, inc=1, device_id=(g, i, j), device_id_type=MESH)
    own_a = pltpu.make_async_copy(a_hbm, abuf.at[1], own_sem.at[0])
    own_b = pltpu.make_async_copy(b_hbm, bbuf.at[me], own_sem.at[1])
    offset_a = pltpu.make_async_copy(aoff_hbm, aoff, own_sem.at[2])
    offset_b = pltpu.make_async_copy(boff_hbm, boff, own_sem.at[3])
    for copy in (own_a, own_b, offset_a, offset_b):
        copy.start()

    pl.semaphore_wait(barrier, count - 1)

    after = ahead(r, 1, rows)
    before = ahead(r, rows - 1, rows)
    a_copies = [
        pltpu.make_async_remote_copy(
            src_ref=a_hbm, dst_ref=abuf.at[slot], send_sem=a_send.at[slot], recv_sem=a_recv.at[slot],
            device_id=(g, to, k), device_id_type=MESH,
        )
        for slot, to in ((0, after), (2, before))
    ]
    for copy in a_copies:
        copy.start()
    b_copies = []
    for d, (i, j) in enumerate(peers):
        b_copies.append(
            pltpu.make_async_remote_copy(
                src_ref=b_hbm, dst_ref=bbuf.at[me], send_sem=b_send.at[d], recv_sem=b_recv.at[me],
                device_id=(g, i, j), device_id_type=MESH,
            )
        )
        b_copies[-1].start()

    for copy in (own_a, offset_a, own_b, offset_b):
        copy.wait()
    for copy in a_copies:
        copy.wait_recv()
    for d, (i, j) in enumerate(peers):
        source = i * cols + j
        pltpu.make_async_remote_copy(
            src_ref=b_hbm, dst_ref=bbuf.at[source], send_sem=b_send.at[d], recv_sem=b_recv.at[source],
            device_id=(g, i, j), device_id_type=MESH,
        ).wait_recv()
    padded = jnp.concatenate([abuf[0], abuf[1], abuf[2]], axis=1)
    extent = padded.shape[1]
    segment = pltpu.roll(padded, lax.rem(extent - aoff[0], extent), 1)[:, :SPAN]
    whole = jnp.concatenate([bbuf[p] for p in range(count)], axis=1)
    extent_b = whole.shape[1]
    start = lax.rem(k * NB + boff[0], extent_b)
    segment_b = pltpu.roll(whole, lax.rem(extent_b - start, extent_b), 1)[:, :SPAN]
    segments = jnp.concatenate([segment, segment_b], axis=0)
    octets(segments, base)
    means, scales = window_stats(segments)

    rest = jnp.concatenate([means[:channels], scales[:channels]], axis=0)
    pieces = []
    for _ in range(3):
        pieces.append(rest.astype(jnp.bfloat16).astype(jnp.float32))
        rest = rest - pieces[-1]
    split = jnp.concatenate(pieces, axis=0).T.astype(jnp.bfloat16)
    kinds = 2 * channels
    shape = (3 * kinds, 2 * LANES)
    kind = lax.broadcasted_iota(jnp.int32, shape, 0) % kinds
    wanted = lax.broadcasted_iota(jnp.int32, shape, 1) // LANES * channels

    for c in range(channels):
        hankel(base, ha, c)
        hankel(base, ha, channels + c)
        chosen = jnp.where(kind == wanted + c, 1.0, 0.0).astype(jnp.bfloat16)
        spread_out[c] = jnp.dot(split, chosen, preferred_element_type=jnp.float32)
        for at in range(0, LANES, 16):
            for q in range(NA // LANES):
                row = at + LANES * q
                mean = spread_out[c, row : row + 16, :LANES]
                scale = spread_out[c, row : row + 16, LANES:]
                for m in range(0, M, LANES):
                    w = ha[c, at : at + 16, LANES * q + m : LANES * q + m + LANES]
                    left[row : row + 16, M * c + m : M * c + m + LANES] = ((w - mean) * scale).astype(jnp.bfloat16)
        mean16 = jnp.broadcast_to(means[channels + c : channels + c + 1], (16, NB))
        scale16 = jnp.broadcast_to(scales[channels + c : channels + c + 1], (16, NB))
        for at in range(0, LANES, 16):
            for q in range(M // LANES):
                w = ha[channels + c, at : at + 16, LANES * q : LANES * q + NB]
                row = at + M * c + LANES * q
                right[row : row + 16, :] = ((w - mean16) * scale16).astype(jnp.bfloat16)

    score[...] = jnp.dot(left[...], right[...], preferred_element_type=jnp.float32)
    factor = 1.0 / (channels * M)

    share_b = NB // rows
    per = LANES // share_b
    tiles = NB // LANES
    depth = K // per
    block = lax.broadcasted_iota(jnp.int32, (depth, LANES), 1) // share_b
    own = r // per
    place = r - own * per
    lb_copies = []

    def send_list(to):
        lb_copies.append(
            pltpu.make_async_remote_copy(
                src_ref=blist.at[to], dst_ref=brecv.at[r], send_sem=lb_send.at[len(lb_copies)], recv_sem=lb_recv.at[r],
                device_id=(g, to, k), device_id_type=MESH,
            )
        )
        lb_copies[-1].start()

    for n in range(tiles):
        if n == tiles - 1:
            t = own
        else:
            down = tiles - 1 - n
            t = jnp.where(
                2 * own < tiles - 1,
                jnp.where(own >= down, down - 1, down),
                jnp.where(own <= n, n + 1, n),
            )
        found = jnp.concatenate(top_columns(score, pl.ds(pl.multiple_of(LANES * t, LANES), LANES)), axis=0)
        for u in range(per):
            packed = None
            for v in range(per):
                piece = shifted(found[depth * v : depth * v + depth], (v - u) * share_b)
                packed = piece if packed is None else jnp.where(block == v, piece, packed)
            blist[t * per + u] = packed
        for u in range(per - 1 if n == tiles - 1 else per):
            send_list(t * per + (ahead(place, u + 1, per) if n == tiles - 1 else u))
    brecv[r] = blist[r]

    score_t[...] = score[...].T
    share_a = NA // cols
    for t in range(NA // LANES):
        found = jnp.concatenate(top_columns(score_t, pl.ds(LANES * t, LANES)), axis=0)
        alist[(LANES * t) // share_a, :, (LANES * t) % share_a : (LANES * t) % share_a + LANES] = found
    la_copies = []
    for d in range(1, cols):
        to = across[d]
        la_copies.append(
            pltpu.make_async_remote_copy(
                src_ref=alist.at[to], dst_ref=arecv.at[k], send_sem=la_send.at[d], recv_sem=la_recv.at[k],
                device_id=(g, r, to), device_id_type=MESH,
            )
        )
        la_copies[-1].start()

    held = alist[k]
    best = [held[j : j + 1] for j in range(K)]
    for d in range(1, cols):
        source = across[d]
        pltpu.make_async_remote_copy(
            src_ref=alist.at[source], dst_ref=arecv.at[source], send_sem=la_send.at[d], recv_sem=la_recv.at[source],
            device_id=(g, r, source), device_id_type=MESH,
        ).wait_recv()
        came = arecv[source]
        best = merge_top(best, [came[j : j + 1] for j in range(K)])
    a_out[...] = jnp.concatenate(best, axis=0) * factor

    for d in range(1, rows):
        source = ahead(r, d, rows)
        pltpu.make_async_remote_copy(
            src_ref=blist.at[source], dst_ref=brecv.at[source], send_sem=lb_send.at[d], recv_sem=lb_recv.at[source],
            device_id=(g, source, k), device_id_type=MESH,
        ).wait_recv()
    lists = [brecv[:, j % depth, (j // depth) * share_b : (j // depth + 1) * share_b] for j in range(K)]
    b_out[...] = jnp.concatenate(merge_sublanes(lists), axis=0) * factor

    for copy in a_copies + b_copies + lb_copies + la_copies:
        copy.wait_send()


def local(rows, cols, series_a, series_b, a_offsets, b_offsets):
    channels, length_a = series_a.shape
    length_b = series_b.shape[1]
    count = rows * cols
    share_a = NA // cols
    share_b = NB // rows
    vmem = pl.BlockSpec(memory_space=pltpu.VMEM)
    hbm = pl.BlockSpec(memory_space=pltpu.HBM)
    dma = pltpu.SemaphoreType.DMA
    f32 = jnp.float32
    a_best, b_best = pl.pallas_call(
        functools.partial(kernel, rows, cols),
        out_shape=(
            pltpu.VMEM((K, share_a), f32),
            pltpu.VMEM((K, share_b), f32),
        ),
        in_specs=[hbm] * 4,
        out_specs=(vmem, vmem),
        scratch_shapes=[
            pltpu.SMEM((1,), jnp.int32),
            pltpu.SMEM((1,), jnp.int32),
            pltpu.VMEM((3, channels, length_a), f32),
            pltpu.VMEM((count, channels, length_b), f32),
            pltpu.VMEM((SPAN // LANES, 2 * channels * SUB, LANES), f32),
            pltpu.VMEM((2 * channels, LANES, WIDE), f32),
            pltpu.VMEM((NA, channels * M), jnp.bfloat16),
            pltpu.VMEM((channels * M, NB), jnp.bfloat16),
            pltpu.VMEM((channels, NA, 2 * LANES), f32),
            pltpu.VMEM((NA, NB), f32),
            pltpu.VMEM((NB, NA), f32),
            pltpu.VMEM((cols, K, share_a), f32),
            pltpu.VMEM((rows, K * share_b // LANES, LANES), f32),
            pltpu.VMEM((cols, K, share_a), f32),
            pltpu.VMEM((rows, K * share_b // LANES, LANES), f32),
            dma((4,)),
            dma((3,)),
            dma((3,)),
            dma((count,)),
            dma((count,)),
            dma((cols,)),
            dma((cols,)),
            dma((rows,)),
            dma((rows,)),
        ],
        compiler_params=pltpu.CompilerParams(collective_id=0, has_side_effects=True),
        name="join",
    )(a_offsets, b_offsets, series_a, series_b)
    return (a_best.T, b_best.T[None])


def solution(mesh):
    in_specs = (
        P(None, ("groups", "rows")),
        P(None, ("groups", "rows", "cols")),
        P(("groups", "rows")),
        P(("groups", "cols")),
    )
    out_specs = (P(("groups", "rows", "cols"), None), P(("groups", "cols"), "rows", None))
    body = functools.partial(local, mesh.shape["rows"], mesh.shape["cols"])
    return jax.shard_map(body, mesh=mesh, in_specs=in_specs, out_specs=out_specs, check_vma=False)
```
